32 devices in a mesh: ctx: 8 (over z, y), ep: 4 (over x, core).
Axes of the slice: x: 2, y: 2, z: 4, core: 2. Of those that a mesh axis runs over, the one named last changes fastest.
Arguments:
- tokens: bfloat16 [12288, 2048], P(('ctx', 'ep')), may hold values from -6 to 6
- expert_ids: int32 [12288, 8], P(('ctx', 'ep')), may hold values from 0 to 127, as said below
- gate_codes: int32 [12288, 8], P(('ctx', 'ep')), may hold values from 4096 to 65536
- out_grad: bfloat16 [12288, 2048], P(('ctx', 'ep')), may hold values from -6 to 6
- expert_weights: bfloat16 [2048, 4, 3, 768], P('ctx', 'ep'), may hold values from -0.21875 to 0.21875
Outputs:
- moe_out: bfloat16 [12288, 2048], P(('ctx', 'ep'))
- input_grad: bfloat16 [12288, 2048], P(('ctx', 'ep'))
- weight_grads: float32 [2048, 4, 3, 768], P('ctx', 'ep')
The draws below stay inside these ranges and needn't reach their ends.
Inputs may be any that keep to these rules, and one draw needn't show every extreme that they name: `expert_ids`: each row names 8 different experts. Within each aligned block of 384 rows (the rows of one device), every expert below 4 is named by 1 to 24 rows, and one expert below 4, the same in every block, is named by exactly 24 rows in every block.
All inputs are finite; a program needn't handle non-finite values.
Results may differ from the reference program's by a relative error of at most 0.015.
Values may be sent and summed in bfloat16 or wider, within the bound.
No kernel may reach another device: no remote copies, remote signals or barrier semaphores. Data moves between devices by JAX's collectives and lax.ppermute only.
A program may use at most 128 MiB of HBM per device.

```python
import jax
import jax.numpy as jnp
from jax import lax

D = 2048
FF = 768
EXPERTS = 128
TOPK = 8
TOK_DEV = 384
WAVE = 4
CAP = 24
TOKENS = 12288
N_CTX = 8
N_EP = 4


def draw_expert_ids(key, part):
    blocks = TOKENS // TOK_DEV
    key_hot, key_counts, key_members, key_rest, key_order = jax.random.split(key, 5)
    hot = jax.random.randint(key_hot, (), 0, WAVE)
    counts = jax.random.randint(key_counts, (blocks, WAVE), 1, CAP + 1)
    counts = jnp.where(jnp.arange(WAVE)[None, :] == hot, CAP, counts)
    member_keys = jax.random.split(key_members, blocks * WAVE)
    ranks = jax.vmap(lambda one_key: jax.random.permutation(one_key, TOK_DEV))(member_keys)
    ranks = ranks.reshape(blocks, WAVE, TOK_DEV)
    member = jnp.transpose(ranks < counts[:, :, None], (0, 2, 1))
    rest_keys = jax.random.split(key_rest, blocks * TOK_DEV)
    others = jax.vmap(lambda one_key: jax.random.permutation(one_key, EXPERTS - WAVE)[:TOPK])(rest_keys) + WAVE
    others = others.reshape(blocks, TOK_DEV, TOPK)
    wave_range = jnp.arange(WAVE)
    wave_ids = jnp.where(member, wave_range[None, None, :], EXPERTS + wave_range[None, None, :])
    joined = jnp.sort(jnp.concatenate([wave_ids, others], axis=2), axis=2)[:, :, :TOPK]
    joined = joined.reshape(TOKENS, TOPK)
    order_keys = jax.random.split(key_order, TOKENS)
    shuffled = jax.vmap(lambda one_key, row: jax.random.permutation(one_key, row))(order_keys, joined)
    return shuffled.astype(jnp.int32)


def touch_ends(result, rng, low, top_value):
    longest = result.shape.index(max(result.shape))
    spots = []
    for shift in (0, 1):
        where = [jax.random.randint(jax.random.fold_in(rng, axis), (), 0, length) for axis, length in enumerate(result.shape)]
        where[longest] = (where[longest] + shift) % result.shape[longest]
        spots.append(tuple(where))
    return result.at[spots[0]].set(low).at[spots[1]].set(top_value)


def block_scale(rng, shape, cuts, low, top_value):
    factor_of = 1.0
    for dim, blocks in cuts:
        heights = jax.random.uniform(jax.random.fold_in(jax.random.fold_in(rng, 6), dim), (blocks,), jnp.float32, low / len(cuts), top_value / len(cuts))
        factor_of = factor_of * jnp.repeat(jnp.exp(heights), shape[dim] // blocks).reshape((-1,) + (1,) * (len(shape) - 1 - dim))
    return factor_of


def gaussian(key, shape, width, most, shards=(), held_as=jnp.bfloat16):
    values = width * jax.random.normal(key, shape, jnp.float32)
    if shards:
        values = values * block_scale(key, shape, shards, -0.22, 0.18)
    return jnp.clip(values, -most, most).astype(held_as)


def setup_inputs(seed: int = 0) -> dict:
    arg_keys = jax.random.split(jax.random.key(seed), 6)
    tokens = gaussian(arg_keys[0], (TOKENS, D), 1.0, 6.0, ((0, 32),))
    expert_ids = draw_expert_ids(jax.random.fold_in(arg_keys[5], 71), 0)
    gate_codes = touch_ends(jax.random.randint(arg_keys[2], (TOKENS, TOPK), 4096, 65537), jax.random.fold_in(arg_keys[2], 1), 4096, 65536).astype(jnp.int32)
    out_grad = gaussian(arg_keys[3], (TOKENS, D), 1.0, 6.0, ((0, 32),))
    expert_weights = gaussian(arg_keys[4], (D, WAVE, 3, FF), FF ** -0.5, 0.21875, ((0, 8), (1, 4)))
    return {"tokens": tokens, "expert_ids": expert_ids, "gate_codes": gate_codes, "out_grad": out_grad, "expert_weights": expert_weights}


def reference(tokens, expert_ids, gate_codes, out_grad, expert_weights):
    blocks = TOKENS // TOK_DEV
    gates = gate_codes.astype(jnp.float32) / 65536.0
    moe = jnp.zeros((TOKENS, D), jnp.float32)
    input_grad = jnp.zeros((TOKENS, D), jnp.float32)
    tok_index = jnp.arange(TOK_DEV, dtype=jnp.int32)
    slot_index = jnp.arange(CAP, dtype=jnp.int32)
    block_start = jnp.arange(blocks, dtype=jnp.int32) * TOK_DEV
    grad_list = []
    for expert in range(WAVE):
        chosen = expert_ids == expert
        member = jnp.any(chosen, axis=1).reshape(blocks, TOK_DEV)
        weight = jnp.sum(jnp.where(chosen, gates, jnp.zeros((), gates.dtype)), axis=1)
        position = jnp.cumsum(member.astype(jnp.int32), axis=1).astype(jnp.int32) - 1
        placed = member[:, :, None] & (position[:, :, None] == slot_index[None, None, :])
        source = jnp.sum(jnp.where(placed, tok_index[None, :, None], 0), axis=1).astype(jnp.int32)
        filled = jnp.any(placed, axis=1).reshape(-1)
        flat = (source + block_start[:, None]).reshape(-1).astype(jnp.int32)
        rows_x = jnp.where(filled[:, None], tokens[flat], jnp.zeros((), tokens.dtype))
        rows_w = jnp.where(filled, weight[flat], jnp.zeros((), weight.dtype))
        route_grad = (rows_w[:, None] * out_grad[flat].astype(jnp.float32)).astype(jnp.bfloat16)
        w_gate = expert_weights[:, expert, 0, :]
        w_up = expert_weights[:, expert, 1, :]
        w_down = expert_weights[:, expert, 2, :]
        pre_gate = jnp.dot(rows_x, w_gate, preferred_element_type=jnp.float32)
        pre_up = jnp.dot(rows_x, w_up, preferred_element_type=jnp.float32)
        soft = jax.nn.sigmoid(pre_gate)
        active = pre_gate * soft
        hidden = (active * pre_up).astype(jnp.bfloat16)
        expert_out = jnp.dot(hidden, w_down.T, preferred_element_type=jnp.float32).astype(jnp.bfloat16)
        moe = moe.at[flat].add(rows_w[:, None] * expert_out.astype(jnp.float32))
        hidden_grad = jnp.dot(route_grad, w_down, preferred_element_type=jnp.float32)
        gate_grad = (hidden_grad * pre_up * soft * (1.0 + pre_gate * (1.0 - soft))).astype(jnp.bfloat16)
        up_grad = (hidden_grad * active).astype(jnp.bfloat16)
        route_input = (jnp.dot(gate_grad, w_gate.T, preferred_element_type=jnp.float32)
                       + jnp.dot(up_grad, w_up.T, preferred_element_type=jnp.float32)).astype(jnp.bfloat16)
        input_grad = input_grad.at[flat].add(route_input.astype(jnp.float32))
        group_rows = N_EP * CAP
        pieces = (rows_x.reshape(N_CTX, group_rows, D), gate_grad.reshape(N_CTX, group_rows, FF),
                  up_grad.reshape(N_CTX, group_rows, FF), route_grad.reshape(N_CTX, group_rows, D),
                  hidden.reshape(N_CTX, group_rows, FF))

        def add_group(total, piece):
            x_group, gate_group, up_group, grad_group, hidden_group = piece
            partial_sum = jnp.stack([
                jnp.dot(x_group.T, gate_group, preferred_element_type=jnp.float32),
                jnp.dot(x_group.T, up_group, preferred_element_type=jnp.float32),
                jnp.dot(grad_group.T, hidden_group, preferred_element_type=jnp.float32)], axis=1)
            return total + partial_sum.astype(jnp.bfloat16).astype(jnp.float32), None

        total, _ = lax.scan(add_group, jnp.zeros((D, 3, FF), jnp.float32), pieces)
        grad_list.append(total)
    weight_grads = jnp.stack(grad_list, axis=1)
    return moe.astype(jnp.bfloat16), input_grad.astype(jnp.bfloat16), weight_grads
```

```python
import jax
import jax.numpy as jnp
from jax import lax
from jax.sharding import PartitionSpec as P

CAP = 24
F32 = jnp.float32
BF16 = jnp.bfloat16


def dot_nn(a, b):
    return lax.dot_general(a, b, (((1,), (0,)), ((), ())), preferred_element_type=F32)


def dot_nt(a, b):
    return lax.dot_general(a, b, (((1,), (1,)), ((), ())), preferred_element_type=F32)


def dot_tn(a, b):
    return lax.dot_general(a, b, (((0,), (0,)), ((), ())), preferred_element_type=F32)


def body(tokens, expert_ids, gate_codes, out_grad, expert_weights):
    n_ep = lax.axis_size("ep")
    n_ctx = lax.axis_size("ctx")
    n_hi = n_ctx // 2
    n_tok, width = tokens.shape
    d_own, _, _, ff = expert_weights.shape
    rows = n_ep * CAP
    odd = lax.axis_index("ctx") % 2 == 1
    pair = [(c, c ^ 1) for c in range(n_ctx)]
    lines = [[2 * h + low for h in range(n_hi)] for low in range(2)]

    def swap(x):
        return lax.ppermute(x, "ctx", pair)

    def over_line(x):
        return lax.all_to_all(
            x, "ctx", split_axis=0, concat_axis=0, axis_index_groups=lines, tiled=True
        )

    def over_ep(x):
        return lax.all_to_all(x, "ep", split_axis=0, concat_axis=0, tiled=True)

    own = [expert_weights[:, 0, k, :] for k in range(3)]
    peer = [None] * 3
    for k in (2, 0, 1):
        peer[k] = swap(own[k])

    gates = gate_codes.astype(F32) / 65536.0
    wave_range = jnp.arange(n_ep, dtype=jnp.int32)
    chosen = expert_ids[:, :, None] == wave_range[None, None, :]
    member = jnp.any(chosen, axis=1)
    route_weight = jnp.sum(jnp.where(chosen, gates[:, :, None], 0.0), axis=1)
    position = jnp.cumsum(member.astype(jnp.int32), axis=0) - 1
    placed = member[:, :, None] & (
        position[:, :, None] == jnp.arange(CAP, dtype=jnp.int32)[None, None, :]
    )
    onehot = placed.astype(BF16).reshape(n_tok, rows)
    slot_weight = jnp.sum(jnp.where(placed, route_weight[:, :, None], 0.0), axis=0)

    def arrange(x):
        x = x.reshape(rows, n_hi, 2, d_own)
        x = jnp.where(odd, x[:, :, ::-1, :], x)
        return x.reshape(rows, n_hi, 2 * d_own)

    def dispatch(x):
        x = over_ep(arrange(x))
        x = over_line(jnp.transpose(x, (1, 0, 2)))
        return x.reshape(n_hi * rows, 2 * d_own)

    slot_grad = (slot_weight.reshape(rows, 1) * dot_tn(onehot, out_grad)).astype(BF16)
    slot_rows = dot_tn(onehot, tokens).astype(BF16)
    g_all = dispatch(slot_grad)
    x_all = dispatch(slot_rows)

    def partial_sum(a, k):
        part = dot_nn(a[:, :d_own], own[k]) + dot_nn(a[:, d_own:], peer[k])
        part = over_line(part.astype(BF16).reshape(n_hi, rows, ff))
        return jnp.sum(part.astype(F32), axis=0)

    hidden_grad = partial_sum(g_all, 2)
    pre_gate = partial_sum(x_all, 0)
    pre_up = partial_sum(x_all, 1)
    soft = jax.nn.sigmoid(pre_gate)
    active = pre_gate * soft
    hidden = (active * pre_up).astype(BF16)
    gate_grad = (hidden_grad * pre_up * soft * (1.0 + pre_gate * (1.0 - soft))).astype(BF16)
    up_grad = (hidden_grad * active).astype(BF16)

    def gather(x):
        x = jnp.broadcast_to(x[None], (n_hi, rows, ff))
        return over_line(x).reshape(n_hi * rows, ff)

    hidden_all = gather(hidden)
    gate_all = gather(gate_grad)
    up_all = gather(up_grad)

    x_own, x_peer = x_all[:, :d_own], x_all[:, d_own:]
    g_own, g_peer = g_all[:, :d_own], g_all[:, d_own:]

    def give_back(first, second):
        x = jnp.concatenate([first, second], axis=1).astype(BF16)
        x = over_line(x.reshape(n_hi, rows, 2 * d_own))
        x = over_ep(jnp.transpose(x, (1, 0, 2)))
        x = x.reshape(rows, n_hi, 2, d_own)
        x = jnp.where(odd, x[:, :, ::-1, :], x)
        return x.reshape(rows, width)

    out_back = give_back(dot_nt(hidden_all, own[2]), dot_nt(hidden_all, peer[2]))
    down_peer = swap(dot_tn(g_peer, hidden_all).astype(BF16))
    input_back = give_back(
        dot_nt(gate_all, own[0]) + dot_nt(up_all, own[1]),
        dot_nt(gate_all, peer[0]) + dot_nt(up_all, peer[1]),
    )
    gate_peer = swap(dot_tn(x_peer, gate_all).astype(BF16))
    up_peer = swap(dot_tn(x_peer, up_all).astype(BF16))
    weight_grads = jnp.stack(
        [
            dot_tn(x_own, gate_all) + gate_peer.astype(F32),
            dot_tn(x_own, up_all) + up_peer.astype(F32),
            dot_tn(g_own, hidden_all) + down_peer.astype(F32),
        ],
        axis=1,
    )[:, None]

    combined = jnp.zeros((n_tok, width), F32)
    for expert in range(n_ep):
        part = slice(expert * CAP, (expert + 1) * CAP)
        picked = dot_nn(onehot[:, part], out_back[part])
        combined = combined + route_weight[:, expert : expert + 1] * picked
    input_grad = dot_nn(onehot, input_back)
    return combined.astype(BF16), input_grad.astype(BF16), weight_grads


def solution(mesh):
    by_token = P(("ctx", "ep"), None)
    by_weight = P("ctx", "ep", None, None)
    return jax.shard_map(
        body,
        mesh=mesh,
        in_specs=(by_token, by_token, by_token, by_token, by_weight),
        out_specs=(by_token, by_token, by_weight),
        check_vma=False,
    )
```

```python
import functools

import jax
import jax.numpy as jnp
from jax import lax
from jax.experimental import pallas as pl
from jax.experimental.pallas import tpu as pltpu
from jax.sharding import PartitionSpec as P

CAP = 24
F32 = jnp.float32
BF16 = jnp.bfloat16
VMEM = pl.BlockSpec(memory_space=pltpu.VMEM)
SMEM = pl.BlockSpec(memory_space=pltpu.SMEM)


def dot(a, b, ca, cb):
    return lax.dot_general(a, b, (((ca,), (cb,)), ((), ())), preferred_element_type=F32)


def shape(dims, dtype=BF16):
    return jax.ShapeDtypeStruct(tuple(dims), dtype)


def call(kernel, name, outs, args, flops=0, scratch=(), n_smem=0):
    moved = sum(a.size * a.dtype.itemsize for a in list(args) + list(outs))
    return pl.pallas_call(
        kernel,
        name=name,
        out_shape=list(outs),
        in_specs=[SMEM] * n_smem + [VMEM] * (len(args) - n_smem),
        out_specs=[VMEM] * len(outs),
        scratch_shapes=list(scratch),
        cost_estimate=pl.CostEstimate(
            flops=int(flops), bytes_accessed=int(moved), transcendentals=0
        ),
    )(*args)


def flip_if(odd, x, d_own):
    flipped = jnp.concatenate([x[:, d_own:], x[:, :d_own]], axis=1)
    return jnp.where(odd, flipped, x)


def scatter_kernel(n_ep, n_hi, d_own, place, ids, codes, tokens, grads, *outs):
    sends, onehot_ref, weight_ref = outs[:n_ep], outs[n_ep], outs[n_ep + 1]
    hi, low, ep = place[0], place[1], place[2]
    n_tok = tokens.shape[0]
    span = 2 * d_own
    members, weights = [], []
    for j in range(n_ep):
        hit = ids[...] == (ep ^ j)
        members.append(jnp.max(jnp.where(hit, 1.0, 0.0), axis=0, keepdims=True))
        code = jnp.sum(jnp.where(hit, codes[...], 0), axis=0, keepdims=True)
        weights.append(code.astype(F32) / 65536.0)
    pad = [jnp.zeros((1, n_tok), F32)] * (-n_ep % 8)
    member = jnp.concatenate(members + pad, axis=0)
    before = lax.broadcasted_iota(jnp.int32, (n_tok, n_tok), 0)
    after = lax.broadcasted_iota(jnp.int32, (n_tok, n_tok), 1)
    upper = jnp.where(before <= after, 1.0, 0.0).astype(BF16)
    count = dot(member.astype(BF16), upper, 1, 0)
    slot = lax.broadcasted_iota(jnp.int32, (CAP, n_tok), 0).astype(F32) + 1.0
    for j in range(n_ep):
        placed = (slot == count[j : j + 1]) & (members[j] > 0.5)
        rows = pl.ds(j * CAP, CAP)
        onehot_ref[rows, :] = jnp.where(placed, 1.0, 0.0).astype(BF16)
        weight_ref[rows, :] = jnp.sum(jnp.where(placed, weights[j], 0.0), axis=1, keepdims=True)
    onehot = onehot_ref[...]
    weight = weight_ref[...]
    odd = low == 1
    for k in range(n_hi):
        cols = pl.ds(pl.multiple_of((hi ^ k) * span, span), span)
        x = flip_if(odd, dot(onehot, tokens[:, cols], 1, 0), d_own)
        g = flip_if(odd, dot(onehot, grads[:, cols], 1, 0) * weight, d_own)
        for j in range(n_ep):
            rows = slice(j * CAP, (j + 1) * CAP)
            sends[j][k, 0] = x[rows].astype(BF16)
            sends[j][k, 1] = g[rows].astype(BF16)


def repack_kernel(n_in, *refs):
    ins, outs = refs[:n_in], refs[n_in:]
    for k, out in enumerate(outs):
        for i, ref in enumerate(ins):
            out[:, i * CAP : (i + 1) * CAP, :] = ref[k]


def unpack_kernel(n_in, *refs):
    ins, outs = refs[:n_in], refs[n_in:]
    for k, ref in enumerate(ins):
        for i, out in enumerate(outs):
            out[k] = ref[:, i * CAP : (i + 1) * CAP, :]


def partial_kernel(n_hi, *refs):
    slots, own, peer, outs = refs[:n_hi], refs[n_hi], refs[n_hi + 1], refs[n_hi + 2 :]
    rows, d_own, ff = slots[0].shape[1], own.shape[1], own.shape[2]
    x = jnp.concatenate([s[0] for s in slots], axis=0)
    g = jnp.concatenate([s[1] for s in slots], axis=0)
    for m, a in enumerate((x, x, g)):
        part = dot(a[:, :d_own], own[m], 1, 0) + dot(a[:, d_own:], peer[m], 1, 0)
        for k in range(n_hi):
            block = part[k * rows : (k + 1) * rows]
            outs[k][:, m * ff : (m + 1) * ff] = block.astype(outs[k].dtype)


def add_kernel(a, b, out):
    out[...] = (a[...] + b[...].astype(F32)).astype(out.dtype)


def act_kernel(n_in, *refs):
    ins, out = refs[:n_in], refs[n_in]
    ff = out.shape[1] // 3

    def total(m):
        cols = slice(m * ff, (m + 1) * ff)
        t = ins[0][:, cols]
        for ref in ins[1:]:
            t = t + ref[:, cols].astype(F32)
        return t

    pre_gate, pre_up, hidden_grad = total(0), total(1), total(2)
    soft = jax.nn.sigmoid(pre_gate)
    active = pre_gate * soft
    out[:, :ff] = (active * pre_up).astype(BF16)
    out[:, ff : 2 * ff] = (
        hidden_grad * pre_up * soft * (1.0 + pre_gate * (1.0 - soft))
    ).astype(BF16)
    out[:, 2 * ff :] = (hidden_grad * active).astype(BF16)


def back_kernel(n_hi, *refs):
    acts, own, peer, outs = refs[:n_hi], refs[n_hi], refs[n_hi + 1], refs[n_hi + 2 :]
    rows, d_own, ff = acts[0].shape[0], own.shape[1], own.shape[2]

    def part(m):
        return jnp.concatenate([a[:, m * ff : (m + 1) * ff] for a in acts], axis=0)

    hidden, gate, up = part(0), part(1), part(2)
    for i, w in enumerate((own, peer)):
        cols = slice(i * d_own, (i + 1) * d_own)
        out = dot(hidden, w[2], 1, 1).astype(BF16)
        grad = (dot(gate, w[0], 1, 1) + dot(up, w[1], 1, 1)).astype(BF16)
        for k in range(n_hi):
            outs[k][0, :, cols] = out[k * rows : (k + 1) * rows]
            outs[k][1, :, cols] = grad[k * rows : (k + 1) * rows]


def weight_kernel(n_in, *refs):
    slots, acts, own, peer = refs[:n_in], refs[n_in : 2 * n_in], refs[-2], refs[-1]
    d_own, ff = own.shape[1], own.shape[2]
    x = jnp.concatenate([s[0] for s in slots], axis=0)
    g = jnp.concatenate([s[1] for s in slots], axis=0)

    def part(m):
        return jnp.concatenate([a[:, m * ff : (m + 1) * ff] for a in acts], axis=0)

    for m, (a, h) in enumerate(((x, 1), (x, 2), (g, 0))):
        both = dot(a, part(h), 0, 0)
        own[m] = both[:d_own]
        peer[m] = both[d_own:].astype(BF16)


def combine_kernel(n_ep, n_hi, d_own, place, onehot_ref, weight_ref, *refs):
    backs, moe, grad = refs[:n_ep], refs[n_ep], refs[n_ep + 1]
    hi, odd = place[0], place[1] == 1
    span = 2 * d_own
    onehot, weight = onehot_ref[...], weight_ref[...]
    thrice = jnp.concatenate([onehot] * 3, axis=0)
    for k in range(n_hi):
        cols = pl.ds(pl.multiple_of((hi ^ k) * span, span), span)
        out = jnp.concatenate([b[k, 0].astype(F32) for b in backs], axis=0) * weight
        first = out.astype(BF16)
        rest = out - first.astype(F32)
        second = rest.astype(BF16)
        third = (rest - second.astype(F32)).astype(BF16)
        terms = jnp.concatenate([first, second, third], axis=0)
        moe[:, cols] = flip_if(odd, dot(thrice, terms, 0, 0), d_own).astype(BF16)
        back = jnp.concatenate([b[k, 1].astype(F32) for b in backs], axis=0).astype(BF16)
        grad[:, cols] = flip_if(odd, dot(onehot, back, 0, 0), d_own).astype(BF16)


def body(tokens, expert_ids, gate_codes, out_grad, expert_weights):
    n_ep = lax.axis_size("ep")
    n_ctx = lax.axis_size("ctx")
    n_hi = n_ctx // 2
    n_tok, width = tokens.shape
    d_own, _, _, ff = expert_weights.shape
    span = 2 * d_own
    ctx = lax.axis_index("ctx")
    place = jnp.stack([ctx // 2, ctx % 2, lax.axis_index("ep")]).astype(jnp.int32)
    bits = [1 << b for b in range(n_hi.bit_length() - 1)]

    def over_ctx(x, flip):
        return lax.ppermute(x, "ctx", [(c, c ^ flip) for c in range(n_ctx)])

    def over_line(x, k):
        return over_ctx(x, 2 * k)

    def over_ep(x, j):
        return lax.ppermute(x, "ep", [(e, e ^ j) for e in range(n_ep)])

    own = jnp.transpose(expert_weights[:, 0], (1, 0, 2))
    peer = over_ctx(own, 1)

    send = (n_hi, 2, CAP, span)
    slots_flops = 4 * n_ep * CAP * n_tok * width
    *sends, onehot, weight = call(
        functools.partial(scatter_kernel, n_ep, n_hi, d_own),
        "scatter",
        [shape(send)] * n_ep + [shape((n_ep * CAP, n_tok)), shape((n_ep * CAP, 1), F32)],
        (place, expert_ids.T, gate_codes.T, tokens, out_grad),
        flops=slots_flops,
        n_smem=1,
    )
    half = max(n_ep // 2, 1)
    groups = [list(range(g, g + half)) for g in range(0, n_ep, half)]
    taken = [sends[0]] + [over_ep(sends[j], j) for j in range(1, n_ep)]
    rows = half * CAP
    mat_flops = 2 * n_hi * rows * span * ff

    slots = []
    for group in groups:
        packed = call(
            functools.partial(repack_kernel, half),
            "repack",
            [shape((2, rows, span))] * n_hi,
            [taken[j] for j in group],
        )
        slots.append([packed[0]] + [over_line(packed[k], k) for k in range(1, n_hi)])

    parts = []
    for g in range(len(groups)):
        parts.append(
            call(
                functools.partial(partial_kernel, n_hi),
                "partial",
                [shape((rows, 3 * ff), F32 if k % 2 == 0 else BF16) for k in range(n_hi)],
                (*slots[g], own, peer),
                flops=3 * mat_flops,
            )
        )

    acts = []
    for g in range(len(groups)):
        chunk = list(parts[g])
        last = [chunk[0]]
        for bit in bits:
            sent = [k for k in range(bit, n_hi, 2 * bit)]
            moved = {k: over_line(chunk[k], bit) for k in sent[::-1]}
            for k in sent[::-1]:
                if k == bit:
                    last.append(moved[k])
                else:
                    into = k ^ bit
                    dtype = BF16 if into & (2 * bit) else F32
                    (chunk[into],) = call(
                        add_kernel, "add", [shape((rows, 3 * ff), dtype)], (chunk[into], moved[k])
                    )
        (act,) = call(
            functools.partial(act_kernel, len(last)), "act", [shape((rows, 3 * ff))], last
        )
        held = {0: act}
        for bit in bits[::-1]:
            for k in list(held):
                held[k ^ bit] = over_line(held[k], bit)
        acts.append([held[k] for k in range(n_hi)])

    returns = []
    for g in range(len(groups)):
        backs = call(
            functools.partial(back_kernel, n_hi),
            "back",
            [shape((2, rows, span))] * n_hi,
            (*acts[g], own, peer),
            flops=3 * mat_flops,
        )
        returns.append([backs[0]] + [over_line(backs[k], k) for k in range(1, n_hi)])

    all_slots = sum(slots, [])
    all_acts = sum(acts, [])
    own_grad, peer_grad = call(
        functools.partial(weight_kernel, len(all_slots)),
        "weight",
        [shape((3, d_own, ff), F32), shape((3, d_own, ff))],
        (*all_slots, *all_acts),
        flops=6 * mat_flops,
    )
    peer_grad = over_ctx(peer_grad, 1)
    weight_grads = jnp.transpose(own_grad + peer_grad.astype(F32), (1, 0, 2))[:, None]

    backs = []
    for g, group in enumerate(groups):
        unpacked = call(
            functools.partial(unpack_kernel, n_hi), "unpack", [shape(send)] * half, returns[g]
        )
        backs += [x if j == 0 else over_ep(x, j) for j, x in zip(group, unpacked)]
    moe_out, input_grad = call(
        functools.partial(combine_kernel, n_ep, n_hi, d_own),
        "combine",
        [shape((n_tok, width))] * 2,
        (place, onehot, weight, *backs),
        flops=2 * slots_flops,
        n_smem=1,
    )
    return moe_out, input_grad, weight_grads


def solution(mesh):
    by_token = P(("ctx", "ep"), None)
    by_weight = P("ctx", "ep", None, None)
    return jax.shard_map(
        body,
        mesh=mesh,
        in_specs=(by_token, by_token, by_token, by_token, by_weight),
        out_specs=(by_token, by_token, by_weight),
        check_vma=False,
    )
```
